512 devices in a mesh: cuts: 32 (over x_lo, z, core), strip: 16 (over y, x_hi).
Axes of the slice: x: 4 (x_hi: 2, x_lo: 2; x = x_hi * 2 + x_lo), y: 8, z: 8, core: 2. Of those that a mesh axis runs over, the one named last changes fastest.
Arguments:
- field: float32 [128, 2, 512, 512], P('cuts', None, 'strip'), may hold values from -6 to 6
- phase: float32 [128, 16384], P('cuts', 'strip'), may hold values from -3.140625 to 3.140625
- energy: float32 [128, 16384], P('cuts', 'strip'), may hold values from -4 to 4
- row_bin: int32 [128, 16384], P('cuts', 'strip'), may hold values from 0 to 511, as said below
- col_bin: int32 [128, 16384], P('cuts', 'strip'), may hold values from 0 to 511
Outputs:
- field_out: float32 [128, 2, 512, 512], P('cuts', None, 'strip')
- phase_out: float32 [128, 16384], P('cuts', 'strip')
- energy_out: float32 [128, 16384], P('cuts', 'strip')
The draws below stay inside these ranges and needn't reach their ends.
Inputs may be any that keep to these rules, and one draw needn't show every extreme that they name: `row_bin`: electron j of every slice sits in row strip j // 1024: its row lies in [(j // 1024) * 32, (j // 1024 + 1) * 32).
All inputs are finite; a program needn't handle non-finite values.
Results may differ from the reference program's by a relative error of at most 0.0014.
Values sent between devices are 32-bit elements; how exact they have to be, the bound alone decides.
A program may use at most 64 MiB of HBM per device.

```python
import jax
import jax.numpy as jnp
from jax import lax

NR = 512
NC = 512
E_DEV = 1024
SLICES = 128
ELECTRONS = 16384
STRIP_ROWS = 32


def draw_row_bin(key, part):
    owner = lax.broadcasted_iota(jnp.int32, (SLICES, ELECTRONS), 1) // E_DEV
    offset = jax.random.randint(key, (SLICES, ELECTRONS), 0, STRIP_ROWS, dtype=jnp.int32)
    return owner * STRIP_ROWS + offset


def plant(values, key, low, largest):
    longest = values.shape.index(max(values.shape))
    spots = []
    for shift in (0, 1):
        where = [jax.random.randint(jax.random.fold_in(key, axis), (), 0, length) for axis, length in enumerate(values.shape)]
        where[longest] = (where[longest] + shift) % values.shape[longest]
        spots.append(tuple(where))
    return values.at[spots[0]].set(low).at[spots[1]].set(largest)


def shard_levels(key, dims, split, least, largest):
    factor_of = 1.0
    for dim, parts in split:
        heights = jax.random.uniform(jax.random.fold_in(jax.random.fold_in(key, 6), dim), (parts,), jnp.float32, least / len(split), largest / len(split))
        factor_of = factor_of * jnp.repeat(jnp.exp(heights), dims[dim] // parts).reshape((-1,) + (1,) * (len(dims) - 1 - dim))
    return factor_of


def noise(key, extent, scale, limit, split=(), kind=jnp.bfloat16):
    factor_of = shard_levels(key, extent, split, -0.22, 0.18) if split else 1.0
    entries = jax.random.normal(key, extent, jnp.float32) * scale * factor_of
    return jnp.minimum(jnp.maximum(entries, -limit), limit).astype(kind)


def setup_inputs(seed: int = 0) -> dict:
    key_list = jax.random.split(jax.random.key(seed), 6)
    return {
        "field": noise(key_list[0], (SLICES, 2, NR, NC), 1.0, 6.0, ((0, 32), (2, 16)), jnp.float32),
        "phase": jnp.clip(jax.random.uniform(key_list[1], (SLICES, ELECTRONS), jnp.float32, -3.140625, 3.140625), -3.140625, 3.140625),
        "energy": noise(key_list[2], (SLICES, ELECTRONS), 1.0, 4.0, ((0, 32), (1, 16)), jnp.float32),
        "row_bin": draw_row_bin(jax.random.fold_in(key_list[5], 71), 0),
        "col_bin": plant(jax.random.randint(key_list[4], (SLICES, ELECTRONS), 0, NC), jax.random.fold_in(key_list[4], 1), 0, NC - 1).astype(jnp.int32),
    }


COUPLING = 0.5
DETUNING = 1.0
SOURCE_GAIN = 0.5
CHIRP_TOP = 60.0


def chirp_phase(length):
    freq_index = lax.iota(jnp.int32, length)
    signed = jnp.where(freq_index < length // 2, freq_index, freq_index - length).astype(jnp.float32)
    scaled = signed / (length // 2)
    return CHIRP_TOP * scaled * scaled


def reference(field, phase, energy, row_bin, col_bin):
    grid_bf = lax.optimization_barrier(field.astype(jnp.bfloat16)).astype(jnp.float32)
    slice_index = jnp.arange(SLICES, dtype=jnp.int32)[:, None]
    field_real = grid_bf[slice_index, 0, row_bin, col_bin]
    field_imag = grid_bf[slice_index, 1, row_bin, col_bin]
    energy_out = energy - COUPLING * (field_real * jnp.cos(phase) - field_imag * jnp.sin(phase))
    phase_out = phase + DETUNING * energy_out
    weight_real = lax.optimization_barrier(jnp.cos(phase_out).astype(jnp.bfloat16)).astype(jnp.float32)
    weight_imag = lax.optimization_barrier((-jnp.sin(phase_out)).astype(jnp.bfloat16)).astype(jnp.float32)
    bunching = jnp.zeros((SLICES, 2, NR, NC), jnp.float32)
    bunching = bunching.at[slice_index, 0, row_bin, col_bin].add(weight_real)
    bunching = bunching.at[slice_index, 1, row_bin, col_bin].add(weight_imag)
    driven = field + SOURCE_GAIN * bunching
    wave = lax.complex(driven[:, 0], driven[:, 1])
    spectrum = jnp.fft.fft2(wave, axes=(1, 2))
    phase_grid = chirp_phase(NR)[:, None] + chirp_phase(NC)[None, :]
    propagator = lax.complex(jnp.cos(phase_grid), -jnp.sin(phase_grid))
    result = jnp.fft.ifft2(spectrum * propagator[None], axes=(1, 2))
    diffracted = jnp.stack([jnp.real(result), jnp.imag(result)], axis=1).astype(jnp.float32)
    field_out = jnp.concatenate([jnp.zeros_like(diffracted[:1]), diffracted[:-1]], axis=0)
    return (field_out, phase_out, energy_out)
```

```python
import functools
import math

import jax
import jax.numpy as jnp
import ml_dtypes
import numpy as np
from jax import lax
from jax.experimental import pallas as pl
from jax.experimental.pallas import tpu as pltpu
from jax.sharding import PartitionSpec as P

COUPLING = 0.5
DETUNING = 1.0
SOURCE_GAIN = 0.5
CHIRP_TOP = 60.0
MESH = pl.DeviceIdType.MESH
F32 = jnp.float32
BF16 = jnp.bfloat16


def axis_matrix(length):
    k = np.arange(length)
    q = np.where(k < length // 2, k, k - length) / (length // 2)
    response = np.fft.ifft(np.exp(-1j * CHIRP_TOP * q * q))
    matrix = response[(k[:, None] - k[None, :]) % length]
    both = np.concatenate([matrix.real, matrix.imag], axis=1).astype(np.float32)
    high = both.astype(ml_dtypes.bfloat16)
    low = (both - high.astype(np.float32)).astype(ml_dtypes.bfloat16)
    return high, low


def cos_sin(x):
    n = jnp.floor(x * (2.0 / math.pi) + 0.5)
    r = ((x - n * 1.5703125) - n * 4.837512969970703125e-4) - n * 7.549789948768648e-8
    z = r * r
    s = r + r * z * (-1.6666654611e-1 + z * (8.3321608736e-3 + z * -1.9515295891e-4))
    c = 1.0 - 0.5 * z + z * z * (
        4.166664568298827e-2 + z * (-1.388731625493765e-3 + z * 2.443315711809948e-5)
    )
    turn = n.astype(jnp.int32) & 3
    odd = (turn & 1) == 1
    cosine = jnp.where(odd, s, c)
    sine = jnp.where(odd, c, s)
    cosine = jnp.where((turn == 1) | (turn == 2), -cosine, cosine)
    sine = jnp.where(turn >= 2, -sine, sine)
    return cosine, sine


def split(x):
    high = x.astype(BF16)
    return high, (x - high.astype(F32)).astype(BF16)


def dot(a, b):
    return jnp.dot(a, b, preferred_element_type=F32)


def push(s, first_row, field_ref, phase_ref, energy_ref, row_ref, col_ref, phase_out, energy_out):
    rows = field_ref.shape[2]
    cols = field_ref.shape[3]
    count = phase_ref.shape[1]
    one = pl.ds(s, 1)
    field = field_ref[s].reshape(2 * rows, cols)
    phase = phase_ref[one, :]
    col_hot = jnp.where(
        lax.broadcasted_iota(jnp.int32, (cols, count), 0) == col_ref[one, :], 1.0, 0.0
    ).astype(BF16)
    row_hot = lax.broadcasted_iota(jnp.int32, (rows, count), 0) == row_ref[one, :] - first_row
    picked = dot(field.astype(BF16), col_hot)
    at_real = jnp.sum(jnp.where(row_hot, picked[:rows], 0.0), axis=0, keepdims=True)
    at_imag = jnp.sum(jnp.where(row_hot, picked[rows:], 0.0), axis=0, keepdims=True)
    cosine, sine = cos_sin(phase)
    energy_next = energy_ref[one, :] - COUPLING * (at_real * cosine - at_imag * sine)
    phase_next = phase + DETUNING * energy_next
    energy_out[one, :] = energy_next
    phase_out[one, :] = phase_next
    cosine, sine = cos_sin(phase_next)
    spread = jnp.concatenate(
        [jnp.where(row_hot, cosine, 0.0), jnp.where(row_hot, -sine, 0.0)], axis=0
    ).astype(BF16)
    deposit = lax.dot_general(spread, col_hot, (((1,), (1,)), ((), ())), preferred_element_type=F32)
    return field + SOURCE_GAIN * deposit


def turn_columns(driven, high_ref, low_ref):
    rows = driven.shape[0] // 2
    cols = driven.shape[1]
    high, low = split(driven)
    upper = dot(jnp.concatenate([high, low], axis=0), high_ref[...])
    total = upper[: 2 * rows] + upper[2 * rows :] + dot(high, low_ref[...])
    real = total[:rows, :cols] - total[rows:, cols:]
    imag = total[:rows, cols:] + total[rows:, :cols]
    return real, imag


def kernel(
    n_cuts,
    n_strip,
    field_ref,
    phase_ref,
    energy_ref,
    row_ref,
    col_ref,
    high_ref,
    low_ref,
    out_ref,
    phase_out,
    energy_out,
    turned,
    received,
    mixed,
    go_send,
    go_recv,
    back_send,
    back_recv,
):
    slices, _, rows, cols = field_ref.shape
    quarter = cols * slices // n_strip
    half = n_strip // 2
    groups = half // slices
    cut = lax.axis_index("cuts")
    me = lax.axis_index("strip")
    y, b = me // 2, me % 2
    my_slice = y % slices
    my_quarter = (y // slices) * 2 + b
    last = my_slice == slices - 1

    barrier = pltpu.get_barrier_semaphore()
    for d in range(1, n_strip):
        pl.semaphore_signal(
            barrier, inc=1, device_id={"cuts": cut, "strip": (me + d) % n_strip}, device_id_type=MESH
        )

    @pl.when(cut > 0)
    def _():
        for a in range(groups):
            for e in range(2):
                pl.semaphore_signal(
                    barrier,
                    inc=1,
                    device_id={"cuts": cut - 1, "strip": (a * slices + slices - 1) * 2 + e},
                    device_id_type=MESH,
                )

    sent = []
    for t in range(slices):
        s = (y + t) % slices
        driven = push(
            s, me * rows, field_ref, phase_ref, energy_ref, row_ref, col_ref, phase_out, energy_out
        )
        real, imag = turn_columns(driven, high_ref, low_ref)
        turned[s, 0] = real
        turned[s, 1] = imag
        if t == 0:
            peers = jnp.where(last & (cut < n_cuts - 1), 2 * n_strip - 1, n_strip - 1)
            pl.semaphore_wait(barrier, peers)

        for da in range(groups):
            for db in range(2):
                a = (y // slices + da) % groups
                e = (b + db) % 2
                target = (a * slices + s) * 2 + e
                lanes = pl.ds(pl.multiple_of((a * 2 + e) * quarter, quarter), quarter)
                source = turned.at[s, :, :, lanes]
                place = received.at[:, pl.ds(pl.multiple_of(me * rows, rows), rows), :]
                if t == 0 and da == 0 and db == 0:
                    copy = pltpu.make_async_copy(source, place, go_recv.at[me])
                else:
                    copy = pltpu.make_async_remote_copy(
                        src_ref=source,
                        dst_ref=place,
                        send_sem=go_send.at[t, da * 2 + db],
                        recv_sem=go_recv.at[me],
                        device_id={"cuts": cut, "strip": target},
                        device_id_type=MESH,
                    )
                copy.start()
                sent.append(copy)

    for i in range(n_strip):
        block = received.at[:, pl.ds(i * rows, rows), :]
        pltpu.make_async_copy(block, block, go_recv.at[i]).wait()
    for copy in sent[1:]:
        copy.wait_send()

    high, low = split(received[...])
    high = jnp.concatenate([high[0], high[1]], axis=1)
    low = jnp.concatenate([low[0], low[1]], axis=1)
    here = pl.ds(pl.multiple_of(my_quarter * quarter, quarter), quarter)
    steps = [half // 2]
    for d in range(half // 2 - 1, 0, -1):
        steps += [d, half - d]
    steps += [0]
    span = 2 * rows
    total_rows = high_ref.shape[0]
    for d in steps:
        to_y = (y + d) % half
        chunk = pl.ds(pl.multiple_of(to_y * span, span), span)
        factors = jnp.concatenate(
            [
                high_ref[chunk, :total_rows],
                high_ref[chunk, total_rows:],
                low_ref[chunk, :total_rows],
                low_ref[chunk, total_rows:],
            ],
            axis=0,
        )
        upper = dot(factors, high)
        total = upper[: 2 * span] + upper[2 * span :] + dot(factors[: 2 * span], low)
        mixed[0, chunk, :] = total[:span, :quarter] - total[span:, quarter:]
        mixed[1, chunk, :] = total[:span, quarter:] + total[span:, :quarter]
        for db in range(2):
            e = (b + db) % 2
            target = to_y * 2 + e
            source = mixed.at[:, pl.ds(pl.multiple_of(target * rows, rows), rows), :]

            @pl.when(jnp.logical_not(last))
            def _():
                place = out_ref.at[my_slice + 1, :, :, here]
                if d == 0 and db == 0:
                    pltpu.make_async_copy(source, place, back_recv.at[me]).start()
                else:
                    pltpu.make_async_remote_copy(
                        src_ref=source,
                        dst_ref=place,
                        send_sem=back_send.at[d * 2 + db],
                        recv_sem=back_recv.at[me],
                        device_id={"cuts": cut, "strip": target},
                        device_id_type=MESH,
                    ).start()

            @pl.when(last & (cut < n_cuts - 1))
            def _():
                pltpu.make_async_remote_copy(
                    src_ref=source,
                    dst_ref=out_ref.at[0, :, :, here],
                    send_sem=back_send.at[d * 2 + db],
                    recv_sem=back_recv.at[me],
                    device_id={"cuts": cut + 1, "strip": target},
                    device_id_type=MESH,
                ).start()

    @pl.when(cut == 0)
    def _():
        out_ref[0] = jnp.zeros(out_ref.shape[1:], F32)

    for i in range(n_strip):
        s = (i // 2) % slices
        lanes = pl.ds(((i // 2) // slices * 2 + i % 2) * quarter, quarter)
        block = out_ref.at[(s + 1) % slices, :, :, lanes]
        if s == slices - 1:

            @pl.when(cut > 0)
            def _():
                pltpu.make_async_copy(block, block, back_recv.at[i]).wait()
        else:
            pltpu.make_async_copy(block, block, back_recv.at[i]).wait()

    first = mixed.at[:, pl.ds(0, rows), :]
    for k in range(1, n_strip):

        @pl.when(jnp.logical_not(last) | (cut < n_cuts - 1))
        def _():
            pltpu.make_async_copy(first, first, back_send.at[k]).wait()

    @pl.when(last & (cut < n_cuts - 1))
    def _():
        pltpu.make_async_copy(first, first, back_send.at[0]).wait()


def shards(n_cuts, n_strip, field, phase, energy, row_bin, col_bin):
    slices, _, rows, cols = field.shape
    high, low = axis_matrix(cols)
    quarter = cols * slices // n_strip
    vmem = pl.BlockSpec(memory_space=pltpu.VMEM)
    dma = pltpu.SemaphoreType.DMA
    return pl.pallas_call(
        functools.partial(kernel, n_cuts, n_strip),
        out_shape=(
            jax.ShapeDtypeStruct(field.shape, F32),
            jax.ShapeDtypeStruct(phase.shape, F32),
            jax.ShapeDtypeStruct(energy.shape, F32),
        ),
        in_specs=[vmem] * 7,
        out_specs=(vmem,) * 3,
        scratch_shapes=[
            pltpu.VMEM(field.shape, F32),
            pltpu.VMEM((2, rows * n_strip, quarter), F32),
            pltpu.VMEM((2, rows * n_strip, quarter), F32),
            dma((slices, n_strip // slices)),
            dma((n_strip,)),
            dma((n_strip,)),
            dma((n_strip,)),
        ],
        compiler_params=pltpu.CompilerParams(collective_id=0, has_side_effects=True),
    )(field, phase, energy, row_bin, col_bin, jnp.asarray(high), jnp.asarray(low))


def solution(mesh):
    return jax.shard_map(
        functools.partial(shards, mesh.shape["cuts"], mesh.shape["strip"]),
        mesh=mesh,
        in_specs=(
            P("cuts", None, "strip", None),
            P("cuts", "strip"),
            P("cuts", "strip"),
            P("cuts", "strip"),
            P("cuts", "strip"),
        ),
        out_specs=(P("cuts", None, "strip", None), P("cuts", "strip"), P("cuts", "strip")),
        check_vma=False,
    )
```

```python
import functools
import math

import jax
import jax.numpy as jnp
import ml_dtypes
import numpy as np
from jax import lax
from jax.experimental import pallas as pl
from jax.experimental.pallas import tpu as pltpu
from jax.sharding import PartitionSpec as P

COUPLING = 0.5
DETUNING = 1.0
SOURCE_GAIN = 0.5
CHIRP_TOP = 60.0
MESH = pl.DeviceIdType.MESH
F32 = jnp.float32
BF16 = jnp.bfloat16


def axis_matrix(length):
    k = np.arange(length)
    q = np.where(k < length // 2, k, k - length) / (length // 2)
    response = np.fft.ifft(np.exp(-1j * CHIRP_TOP * q * q))
    matrix = response[(k[:, None] - k[None, :]) % length]
    both = np.concatenate([matrix.real, matrix.imag], axis=1).astype(np.float32)
    high = both.astype(ml_dtypes.bfloat16)
    low = (both - high.astype(np.float32)).astype(ml_dtypes.bfloat16)
    return high, low


def cos_sin(x):
    n = jnp.floor(x * (2.0 / math.pi) + 0.5)
    r = ((x - n * 1.5703125) - n * 4.837512969970703125e-4) - n * 7.549789948768648e-8
    z = r * r
    s = r + r * z * (-1.6666654611e-1 + z * (8.3321608736e-3 + z * -1.9515295891e-4))
    c = 1.0 - 0.5 * z + z * z * (
        4.166664568298827e-2 + z * (-1.388731625493765e-3 + z * 2.443315711809948e-5)
    )
    turn = n.astype(jnp.int32) & 3
    odd = (turn & 1) == 1
    cosine = jnp.where(odd, s, c)
    sine = jnp.where(odd, c, s)
    cosine = jnp.where((turn == 1) | (turn == 2), -cosine, cosine)
    sine = jnp.where(turn >= 2, -sine, sine)
    return cosine, sine


def split(x):
    high = x.astype(BF16)
    return high, (x - high.astype(F32)).astype(BF16)


def dot(a, b):
    return jnp.dot(a, b, preferred_element_type=F32)


def push(s, first_row, field_ref, phase_ref, energy_ref, row_ref, col_ref, phase_out, energy_out):
    rows = field_ref.shape[2]
    cols = field_ref.shape[3]
    count = phase_ref.shape[1]
    one = pl.ds(s, 1)
    field = field_ref[s].reshape(2 * rows, cols)
    phase = phase_ref[one, :]
    col_hot = jnp.where(
        lax.broadcasted_iota(jnp.int32, (cols, count), 0) == col_ref[one, :], 1.0, 0.0
    ).astype(BF16)
    row_hot = lax.broadcasted_iota(jnp.int32, (rows, count), 0) == row_ref[one, :] - first_row
    picked = dot(field.astype(BF16), col_hot)
    at_real = jnp.sum(jnp.where(row_hot, picked[:rows], 0.0), axis=0, keepdims=True)
    at_imag = jnp.sum(jnp.where(row_hot, picked[rows:], 0.0), axis=0, keepdims=True)
    cosine, sine = cos_sin(phase)
    energy_next = energy_ref[one, :] - COUPLING * (at_real * cosine - at_imag * sine)
    phase_next = phase + DETUNING * energy_next
    energy_out[one, :] = energy_next
    phase_out[one, :] = phase_next
    cosine, sine = cos_sin(phase_next)
    spread = jnp.concatenate(
        [jnp.where(row_hot, cosine, 0.0), jnp.where(row_hot, -sine, 0.0)], axis=0
    ).astype(BF16)
    deposit = lax.dot_general(spread, col_hot, (((1,), (1,)), ((), ())), preferred_element_type=F32)
    return field + SOURCE_GAIN * deposit


def turn_columns(driven, high_ref, low_ref):
    rows = driven.shape[0] // 2
    cols = driven.shape[1]
    high, low = split(driven)
    upper = dot(jnp.concatenate([high, low], axis=0), high_ref[...])
    total = upper[: 2 * rows] + upper[2 * rows :] + dot(high, low_ref[...])
    real = total[:rows, :cols] - total[rows:, cols:]
    imag = total[:rows, cols:] + total[rows:, :cols]
    return real, imag


def kernel(
    n_cuts,
    n_strip,
    field_ref,
    phase_ref,
    energy_ref,
    row_ref,
    col_ref,
    high_ref,
    low_ref,
    out_ref,
    phase_out,
    energy_out,
    turned,
    received,
    mixed,
    go_send,
    go_recv,
    back_send,
    back_recv,
):
    slices, _, rows, cols = field_ref.shape
    quarter = cols * slices // n_strip
    half = n_strip // 2
    groups = half // slices
    cut = lax.axis_index("cuts")
    me = lax.axis_index("strip")
    y, b = me // 2, me % 2
    my_slice = y % slices
    my_quarter = (y // slices) * 2 + b
    last = my_slice == slices - 1

    barrier = pltpu.get_barrier_semaphore()
    for d in range(1, n_strip):
        pl.semaphore_signal(
            barrier, inc=1, device_id={"cuts": cut, "strip": (me + d) % n_strip}, device_id_type=MESH
        )

    @pl.when(last & (cut > 0))
    def _():
        for i in range(n_strip):
            pl.semaphore_signal(
                barrier, inc=1, device_id={"cuts": cut - 1, "strip": i}, device_id_type=MESH
            )

    for t in range(slices):
        s = (y + t) % slices
        driven = push(
            s, me * rows, field_ref, phase_ref, energy_ref, row_ref, col_ref, phase_out, energy_out
        )
        real, imag = turn_columns(driven, high_ref, low_ref)
        turned[s, 0] = real
        turned[s, 1] = imag
        if t == 0:
            peers = jnp.where(cut < n_cuts - 1, n_strip - 1 + n_strip // slices, n_strip - 1)
            pl.semaphore_wait(barrier, peers)

        for da in range(groups):
            for db in range(2):
                a = (y // slices + da) % groups
                e = (b + db) % 2
                target = (a * slices + s) * 2 + e
                lanes = pl.ds(pl.multiple_of((a * 2 + e) * quarter, quarter), quarter)
                source = turned.at[s, :, :, lanes]
                place = received.at[:, pl.ds(pl.multiple_of(me * rows, rows), rows), :]
                def send(to_cut):
                    pltpu.make_async_remote_copy(
                        src_ref=source,
                        dst_ref=place,
                        send_sem=go_send.at[t, da * 2 + db],
                        recv_sem=go_recv.at[me],
                        device_id={"cuts": to_cut, "strip": target},
                        device_id_type=MESH,
                    ).start()

                @pl.when((s == slices - 1) & (cut < n_cuts - 1))
                def _():
                    send(cut + 1)

                @pl.when(s < slices - 1)
                def _():
                    if t == 0 and da == 0 and db == 0:
                        pltpu.make_async_copy(source, place, go_recv.at[me]).start()
                    else:
                        send(cut)

    has_slice = jnp.logical_not(last) | (cut > 0)

    @pl.when(has_slice)
    def _():
        for i in range(n_strip):
            block = received.at[:, pl.ds(i * rows, rows), :]
            pltpu.make_async_copy(block, block, go_recv.at[i]).wait()

    @pl.when(jnp.logical_not(has_slice))
    def _():
        received[...] = jnp.zeros(received.shape, F32)

    high, low = split(received[...])
    high = jnp.concatenate([high[0], high[1]], axis=1)
    low = jnp.concatenate([low[0], low[1]], axis=1)
    here = pl.ds(pl.multiple_of(my_quarter * quarter, quarter), quarter)
    steps = [half // 2]
    for d in range(half // 2 - 1, 0, -1):
        steps += [d, half - d]
    steps += [0]
    span = 2 * rows
    total_rows = high_ref.shape[0]
    for d in steps:
        to_y = (y + d) % half
        chunk = pl.ds(pl.multiple_of(to_y * span, span), span)
        factors = jnp.concatenate(
            [
                high_ref[chunk, :total_rows],
                high_ref[chunk, total_rows:],
                low_ref[chunk, :total_rows],
                low_ref[chunk, total_rows:],
            ],
            axis=0,
        )
        upper = dot(factors, high)
        total = upper[: 2 * span] + upper[2 * span :] + dot(factors[: 2 * span], low)
        mixed[0, chunk, :] = total[:span, :quarter] - total[span:, quarter:]
        mixed[1, chunk, :] = total[:span, quarter:] + total[span:, :quarter]
        for db in range(2):
            e = (b + db) % 2
            target = to_y * 2 + e
            source = mixed.at[:, pl.ds(pl.multiple_of(target * rows, rows), rows), :]

            place = out_ref.at[(my_slice + 1) % slices, :, :, here]
            if d == 0 and db == 0:
                pltpu.make_async_copy(source, place, back_recv.at[me]).start()
            else:
                pltpu.make_async_remote_copy(
                    src_ref=source,
                    dst_ref=place,
                    send_sem=back_send.at[d * 2 + db],
                    recv_sem=back_recv.at[me],
                    device_id={"cuts": cut, "strip": target},
                    device_id_type=MESH,
                ).start()

    block = received.at[:, pl.ds(0, rows), :]
    for t in range(slices):
        s = (y + t) % slices
        for k in range(n_strip // slices):
            goes = (s == slices - 1) & (cut < n_cuts - 1)
            if t > 0 or k > 0:
                goes = goes | (s < slices - 1)

            @pl.when(goes)
            def _():
                pltpu.make_async_copy(block, block, go_send.at[t, k]).wait()

    for i in range(n_strip):
        lanes = pl.ds(((i // 2) // slices * 2 + i % 2) * quarter, quarter)
        block = out_ref.at[((i // 2) % slices + 1) % slices, :, :, lanes]
        pltpu.make_async_copy(block, block, back_recv.at[i]).wait()
    block = mixed.at[:, pl.ds(0, rows), :]
    for k in range(1, n_strip):
        pltpu.make_async_copy(block, block, back_send.at[k]).wait()


def shards(n_cuts, n_strip, field, phase, energy, row_bin, col_bin):
    slices, _, rows, cols = field.shape
    high, low = axis_matrix(cols)
    quarter = cols * slices // n_strip
    vmem = pl.BlockSpec(memory_space=pltpu.VMEM)
    dma = pltpu.SemaphoreType.DMA
    return pl.pallas_call(
        functools.partial(kernel, n_cuts, n_strip),
        out_shape=(
            jax.ShapeDtypeStruct(field.shape, F32),
            jax.ShapeDtypeStruct(phase.shape, F32),
            jax.ShapeDtypeStruct(energy.shape, F32),
        ),
        in_specs=[vmem] * 7,
        out_specs=(vmem,) * 3,
        scratch_shapes=[
            pltpu.VMEM(field.shape, F32),
            pltpu.VMEM((2, rows * n_strip, quarter), F32),
            pltpu.VMEM((2, rows * n_strip, quarter), F32),
            dma((slices, n_strip // slices)),
            dma((n_strip,)),
            dma((n_strip,)),
            dma((n_strip,)),
        ],
        compiler_params=pltpu.CompilerParams(collective_id=0, has_side_effects=True),
    )(field, phase, energy, row_bin, col_bin, jnp.asarray(high), jnp.asarray(low))


def solution(mesh):
    return jax.shard_map(
        functools.partial(shards, mesh.shape["cuts"], mesh.shape["strip"]),
        mesh=mesh,
        in_specs=(
            P("cuts", None, "strip", None),
            P("cuts", "strip"),
            P("cuts", "strip"),
            P("cuts", "strip"),
            P("cuts", "strip"),
        ),
        out_specs=(P("cuts", None, "strip", None), P("cuts", "strip"), P("cuts", "strip")),
        check_vma=False,
    )
```

```python
import functools
import math

import jax
import jax.numpy as jnp
import ml_dtypes
import numpy as np
from jax import lax
from jax.experimental import pallas as pl
from jax.experimental.pallas import tpu as pltpu
from jax.sharding import PartitionSpec as P

COUPLING = 0.5
DETUNING = 1.0
SOURCE_GAIN = 0.5
CHIRP_TOP = 60.0
MESH = pl.DeviceIdType.MESH
F32 = jnp.float32
BF16 = jnp.bfloat16


def axis_matrix(length):
    k = np.arange(length)
    q = np.where(k < length // 2, k, k - length) / (length // 2)
    response = np.fft.ifft(np.exp(-1j * CHIRP_TOP * q * q))
    matrix = response[(k[:, None] - k[None, :]) % length]
    both = np.concatenate([matrix.real, matrix.imag], axis=1).astype(np.float32)
    high = both.astype(ml_dtypes.bfloat16)
    low = (both - high.astype(np.float32)).astype(ml_dtypes.bfloat16)
    return high, low


def cos_sin(x):
    n = jnp.floor(x * (2.0 / math.pi) + 0.5)
    r = ((x - n * 1.5703125) - n * 4.837512969970703125e-4) - n * 7.549789948768648e-8
    z = r * r
    s = r + r * z * (-1.6666654611e-1 + z * (8.3321608736e-3 + z * -1.9515295891e-4))
    c = 1.0 - 0.5 * z + z * z * (
        4.166664568298827e-2 + z * (-1.388731625493765e-3 + z * 2.443315711809948e-5)
    )
    turn = n.astype(jnp.int32) & 3
    odd = (turn & 1) == 1
    cosine = jnp.where(odd, s, c)
    sine = jnp.where(odd, c, s)
    cosine = jnp.where((turn == 1) | (turn == 2), -cosine, cosine)
    sine = jnp.where(turn >= 2, -sine, sine)
    return cosine, sine


def split(x):
    high = x.astype(BF16)
    return high, (x - high.astype(F32)).astype(BF16)


def dot(a, b):
    return jnp.dot(a, b, preferred_element_type=F32)


def push(s, first_row, field_ref, phase_ref, energy_ref, row_ref, col_ref, phase_out, energy_out):
    rows = field_ref.shape[2]
    cols = field_ref.shape[3]
    count = phase_ref.shape[1]
    one = pl.ds(s, 1)
    field = field_ref[s].reshape(2 * rows, cols)
    phase = phase_ref[one, :]
    col_hot = jnp.where(
        lax.broadcasted_iota(jnp.int32, (cols, count), 0) == col_ref[one, :], 1.0, 0.0
    ).astype(BF16)
    row_hot = lax.broadcasted_iota(jnp.int32, (rows, count), 0) == row_ref[one, :] - first_row
    picked = dot(field.astype(BF16), col_hot)
    at_real = jnp.sum(jnp.where(row_hot, picked[:rows], 0.0), axis=0, keepdims=True)
    at_imag = jnp.sum(jnp.where(row_hot, picked[rows:], 0.0), axis=0, keepdims=True)
    cosine, sine = cos_sin(phase)
    energy_next = energy_ref[one, :] - COUPLING * (at_real * cosine - at_imag * sine)
    phase_next = phase + DETUNING * energy_next
    energy_out[one, :] = energy_next
    phase_out[one, :] = phase_next
    cosine, sine = cos_sin(phase_next)
    spread = jnp.concatenate(
        [jnp.where(row_hot, cosine, 0.0), jnp.where(row_hot, -sine, 0.0)], axis=0
    ).astype(BF16)
    deposit = lax.dot_general(spread, col_hot, (((1,), (1,)), ((), ())), preferred_element_type=F32)
    return field + SOURCE_GAIN * deposit


def turn_columns(driven, high_ref, low_ref):
    rows = driven.shape[0] // 2
    cols = driven.shape[1]
    high, low = split(driven)
    upper = dot(jnp.concatenate([high, low], axis=0), high_ref[...])
    total = upper[: 2 * rows] + upper[2 * rows :] + dot(high, low_ref[...])
    real = total[:rows, :cols] - total[rows:, cols:]
    imag = total[:rows, cols:] + total[rows:, :cols]
    return real, imag


def kernel(
    n_cuts,
    n_strip,
    field_ref,
    phase_ref,
    energy_ref,
    row_ref,
    col_ref,
    high_in,
    low_in,
    out_ref,
    phase_out,
    energy_out,
    high_ref,
    low_ref,
    turned,
    received,
    mixed,
    table_sem,
    go_send,
    go_recv,
    back_send,
    back_recv,
):
    slices, _, rows, cols = field_ref.shape
    quarter = cols * slices // n_strip
    half = n_strip // 2
    groups = half // slices
    tables = [
        pltpu.make_async_copy(high_in, high_ref, table_sem.at[0]),
        pltpu.make_async_copy(low_in, low_ref, table_sem.at[1]),
    ]
    for table in tables:
        table.start()
    cut = lax.axis_index("cuts")
    me = lax.axis_index("strip")
    y, b = me // 2, me % 2
    my_slice = y % slices
    my_quarter = (y // slices) * 2 + b
    last = my_slice == slices - 1

    barrier = pltpu.get_barrier_semaphore()
    for d in range(1, n_strip):
        pl.semaphore_signal(
            barrier, inc=1, device_id={"cuts": cut, "strip": (me + d) % n_strip}, device_id_type=MESH
        )

    @pl.when(last & (cut > 0))
    def _():
        for i in range(n_strip):
            pl.semaphore_signal(
                barrier, inc=1, device_id={"cuts": cut - 1, "strip": i}, device_id_type=MESH
            )

    for t in range(slices):
        s = (y + t) % slices
        driven = push(
            s, me * rows, field_ref, phase_ref, energy_ref, row_ref, col_ref, phase_out, energy_out
        )
        if t == 0:
            for table in tables:
                table.wait()
        real, imag = turn_columns(driven, high_ref, low_ref)
        turned[s, 0] = real
        turned[s, 1] = imag
        if t == 0:
            peers = jnp.where(cut < n_cuts - 1, n_strip - 1 + n_strip // slices, n_strip - 1)
            pl.semaphore_wait(barrier, peers)

        for da in range(groups):
            for db in range(2):
                a = (y // slices + da) % groups
                e = (b + db) % 2
                target = (a * slices + s) * 2 + e
                lanes = pl.ds(pl.multiple_of((a * 2 + e) * quarter, quarter), quarter)
                source = turned.at[s, :, :, lanes]
                place = received.at[:, pl.ds(pl.multiple_of(me * rows, rows), rows), :]
                def send(to_cut):
                    pltpu.make_async_remote_copy(
                        src_ref=source,
                        dst_ref=place,
                        send_sem=go_send.at[t, da * 2 + db],
                        recv_sem=go_recv.at[me],
                        device_id={"cuts": to_cut, "strip": target},
                        device_id_type=MESH,
                    ).start()

                @pl.when((s == slices - 1) & (cut < n_cuts - 1))
                def _():
                    send(cut + 1)

                @pl.when(s < slices - 1)
                def _():
                    if t == 0 and da == 0 and db == 0:
                        pltpu.make_async_copy(source, place, go_recv.at[me]).start()
                    else:
                        send(cut)

    has_slice = jnp.logical_not(last) | (cut > 0)

    @pl.when(has_slice)
    def _():
        for i in range(n_strip):
            block = received.at[:, pl.ds(i * rows, rows), :]
            pltpu.make_async_copy(block, block, go_recv.at[i]).wait()

    @pl.when(jnp.logical_not(has_slice))
    def _():
        received[...] = jnp.zeros(received.shape, F32)

    high, low = split(received[...])
    high = jnp.concatenate([high[0], high[1]], axis=1)
    low = jnp.concatenate([low[0], low[1]], axis=1)
    here = pl.ds(pl.multiple_of(my_quarter * quarter, quarter), quarter)
    steps = [half // 2]
    for d in range(half // 2 - 1, 0, -1):
        steps += [d, half - d]
    steps += [0]
    span = 2 * rows
    total_rows = high_ref.shape[0]
    for d in steps:
        to_y = (y + d) % half
        chunk = pl.ds(pl.multiple_of(to_y * span, span), span)
        factors = jnp.concatenate(
            [
                high_ref[chunk, :total_rows],
                high_ref[chunk, total_rows:],
                low_ref[chunk, :total_rows],
                low_ref[chunk, total_rows:],
            ],
            axis=0,
        )
        upper = dot(factors, high)
        total = upper[: 2 * span] + upper[2 * span :] + dot(factors[: 2 * span], low)
        mixed[0, chunk, :] = total[:span, :quarter] - total[span:, quarter:]
        mixed[1, chunk, :] = total[:span, quarter:] + total[span:, :quarter]
        for db in range(2):
            e = (b + db) % 2
            target = to_y * 2 + e
            source = mixed.at[:, pl.ds(pl.multiple_of(target * rows, rows), rows), :]

            place = out_ref.at[(my_slice + 1) % slices, :, :, here]
            if d == 0 and db == 0:
                pltpu.make_async_copy(source, place, back_recv.at[me]).start()
            else:
                pltpu.make_async_remote_copy(
                    src_ref=source,
                    dst_ref=place,
                    send_sem=back_send.at[d * 2 + db],
                    recv_sem=back_recv.at[me],
                    device_id={"cuts": cut, "strip": target},
                    device_id_type=MESH,
                ).start()

    block = received.at[:, pl.ds(0, rows), :]
    for t in range(slices):
        s = (y + t) % slices
        for k in range(n_strip // slices):
            goes = (s == slices - 1) & (cut < n_cuts - 1)
            if t > 0 or k > 0:
                goes = goes | (s < slices - 1)

            @pl.when(goes)
            def _():
                pltpu.make_async_copy(block, block, go_send.at[t, k]).wait()

    for i in range(n_strip):
        lanes = pl.ds(((i // 2) // slices * 2 + i % 2) * quarter, quarter)
        block = out_ref.at[((i // 2) % slices + 1) % slices, :, :, lanes]
        pltpu.make_async_copy(block, block, back_recv.at[i]).wait()
    block = mixed.at[:, pl.ds(0, rows), :]
    for k in range(1, n_strip):
        pltpu.make_async_copy(block, block, back_send.at[k]).wait()


def hand_out(field, phase, energy, field_out, phase_out, energy_out, sem):
    copies = [
        pltpu.make_async_copy(a, b, sem.at[i])
        for i, (a, b) in enumerate(
            ((field, field_out), (phase, phase_out), (energy, energy_out))
        )
    ]
    for copy in copies:
        copy.start()
    for copy in copies:
        copy.wait()


def shards(n_cuts, n_strip, field, phase, energy, row_bin, col_bin):
    slices, _, rows, cols = field.shape
    high, low = axis_matrix(cols)
    quarter = cols * slices // n_strip
    vmem = pl.BlockSpec(memory_space=pltpu.VMEM)
    dma = pltpu.SemaphoreType.DMA
    moved = pl.pallas_call(
        functools.partial(kernel, n_cuts, n_strip),
        out_shape=(
            pltpu.VMEM(field.shape, F32),
            pltpu.VMEM(phase.shape, F32),
            pltpu.VMEM(energy.shape, F32),
        ),
        in_specs=[vmem] * 5 + [pl.BlockSpec(memory_space=pl.ANY)] * 2,
        out_specs=(vmem,) * 3,
        scratch_shapes=[
            pltpu.VMEM(high.shape, BF16),
            pltpu.VMEM(low.shape, BF16),
            pltpu.VMEM(field.shape, F32),
            pltpu.VMEM((2, rows * n_strip, quarter), F32),
            pltpu.VMEM((2, rows * n_strip, quarter), F32),
            dma((2,)),
            dma((slices, n_strip // slices)),
            dma((n_strip,)),
            dma((n_strip,)),
            dma((n_strip,)),
        ],
        compiler_params=pltpu.CompilerParams(collective_id=0, has_side_effects=True),
    )(field, phase, energy, row_bin, col_bin, jnp.asarray(high), jnp.asarray(low))
    return pl.pallas_call(
        hand_out,
        out_shape=tuple(jax.ShapeDtypeStruct(x.shape, x.dtype) for x in moved),
        in_specs=[pl.BlockSpec(memory_space=pltpu.VMEM)] * 3,
        out_specs=(pl.BlockSpec(memory_space=pl.ANY),) * 3,
        scratch_shapes=[dma((3,))],
    )(*(pltpu.with_memory_space_constraint(x, pltpu.VMEM) for x in moved))


def solution(mesh):
    return jax.shard_map(
        functools.partial(shards, mesh.shape["cuts"], mesh.shape["strip"]),
        mesh=mesh,
        in_specs=(
            P("cuts", None, "strip", None),
            P("cuts", "strip"),
            P("cuts", "strip"),
            P("cuts", "strip"),
            P("cuts", "strip"),
        ),
        out_specs=(P("cuts", None, "strip", None), P("cuts", "strip"), P("cuts", "strip")),
        check_vma=False,
    )
```

```python
import functools
import math

import jax
import jax.numpy as jnp
import ml_dtypes
import numpy as np
from jax import lax
from jax.experimental import pallas as pl
from jax.experimental.pallas import tpu as pltpu
from jax.sharding import PartitionSpec as P

COUPLING = 0.5
DETUNING = 1.0
SOURCE_GAIN = 0.5
CHIRP_TOP = 60.0
MESH = pl.DeviceIdType.MESH
F32 = jnp.float32
BF16 = jnp.bfloat16


def axis_matrix(length):
    k = np.arange(length)
    q = np.where(k < length // 2, k, k - length) / (length // 2)
    response = np.fft.ifft(np.exp(-1j * CHIRP_TOP * q * q))
    matrix = response[(k[:, None] - k[None, :]) % length]
    both = np.concatenate([matrix.real, matrix.imag], axis=1).astype(np.float32)
    high = both.astype(ml_dtypes.bfloat16)
    low = (both - high.astype(np.float32)).astype(ml_dtypes.bfloat16)
    return high, low


def cos_sin(x):
    n = jnp.floor(x * (2.0 / math.pi) + 0.5)
    r = ((x - n * 1.5703125) - n * 4.837512969970703125e-4) - n * 7.549789948768648e-8
    z = r * r
    s = r + r * z * (-1.6666654611e-1 + z * (8.3321608736e-3 + z * -1.9515295891e-4))
    c = 1.0 - 0.5 * z + z * z * (
        4.166664568298827e-2 + z * (-1.388731625493765e-3 + z * 2.443315711809948e-5)
    )
    turn = n.astype(jnp.int32) & 3
    odd = (turn & 1) == 1
    cosine = jnp.where(odd, s, c)
    sine = jnp.where(odd, c, s)
    cosine = jnp.where((turn == 1) | (turn == 2), -cosine, cosine)
    sine = jnp.where(turn >= 2, -sine, sine)
    return cosine, sine


def split(x):
    high = x.astype(BF16)
    return high, (x - high.astype(F32)).astype(BF16)


def dot(a, b):
    return jnp.dot(a, b, preferred_element_type=F32)


def push(s, first_row, field_ref, phase_ref, energy_ref, row_ref, col_ref, phase_out, energy_out):
    rows = field_ref.shape[2]
    cols = field_ref.shape[3]
    count = phase_ref.shape[1]
    one = pl.ds(s, 1)
    field = field_ref[s].reshape(2 * rows, cols)
    phase = phase_ref[one, :]
    col_hot = jnp.where(
        lax.broadcasted_iota(jnp.int32, (cols, count), 0) == col_ref[one, :], 1.0, 0.0
    ).astype(BF16)
    row_hot = lax.broadcasted_iota(jnp.int32, (rows, count), 0) == row_ref[one, :] - first_row
    picked = dot(field.astype(BF16), col_hot)
    at_real = jnp.sum(jnp.where(row_hot, picked[:rows], 0.0), axis=0, keepdims=True)
    at_imag = jnp.sum(jnp.where(row_hot, picked[rows:], 0.0), axis=0, keepdims=True)
    cosine, sine = cos_sin(phase)
    energy_next = energy_ref[one, :] - COUPLING * (at_real * cosine - at_imag * sine)
    phase_next = phase + DETUNING * energy_next
    energy_out[one, :] = energy_next
    phase_out[one, :] = phase_next
    cosine, sine = cos_sin(phase_next)
    spread = jnp.concatenate(
        [jnp.where(row_hot, cosine, 0.0), jnp.where(row_hot, -sine, 0.0)], axis=0
    ).astype(BF16)
    deposit = lax.dot_general(spread, col_hot, (((1,), (1,)), ((), ())), preferred_element_type=F32)
    return field + SOURCE_GAIN * deposit


def turn_columns(driven, high_ref, low_ref):
    rows = driven.shape[0] // 2
    cols = driven.shape[1]
    high, low = split(driven)
    upper = dot(jnp.concatenate([high, low], axis=0), high_ref[...])
    total = upper[: 2 * rows] + upper[2 * rows :] + dot(high, low_ref[...])
    real = total[:rows, :cols] - total[rows:, cols:]
    imag = total[:rows, cols:] + total[rows:, :cols]
    return real, imag


def kernel(
    n_cuts,
    n_strip,
    field_in,
    phase_in,
    energy_in,
    row_in,
    col_in,
    high_in,
    low_in,
    out_ref,
    phase_out,
    energy_out,
    field_ref,
    phase_ref,
    energy_ref,
    row_ref,
    col_ref,
    high_ref,
    low_ref,
    turned,
    received,
    upper_half,
    lower_half,
    mixed,
    load_sem,
    field_sem,
    go_send,
    go_recv,
    back_send,
    back_recv,
):
    slices, _, rows, cols = field_in.shape
    quarter = cols * slices // n_strip
    half = n_strip // 2
    groups = half // slices
    cut = lax.axis_index("cuts")
    me = lax.axis_index("strip")
    y, b = me // 2, me % 2
    my_slice = y % slices
    my_quarter = (y // slices) * 2 + b
    last = my_slice == slices - 1

    barrier = pltpu.get_barrier_semaphore()
    for d in range(1, n_strip):
        pl.semaphore_signal(
            barrier, inc=1, device_id={"cuts": cut, "strip": (me + d) % n_strip}, device_id_type=MESH
        )

    @pl.when(last & (cut > 0))
    def _():
        for i in range(n_strip):
            pl.semaphore_signal(
                barrier, inc=1, device_id={"cuts": cut - 1, "strip": i}, device_id_type=MESH
            )

    electrons = [
        pltpu.make_async_copy(a, b, load_sem.at[i])
        for i, (a, b) in enumerate(
            (
                (phase_in, phase_ref),
                (energy_in, energy_ref),
                (row_in, row_ref),
                (col_in, col_ref),
            )
        )
    ]
    fields = [
        pltpu.make_async_copy(
            field_in.at[(y + t) % slices], field_ref.at[(y + t) % slices], field_sem.at[t]
        )
        for t in range(slices)
    ]
    tables = [
        pltpu.make_async_copy(high_in, high_ref, load_sem.at[4]),
        pltpu.make_async_copy(low_in, low_ref, load_sem.at[5]),
    ]
    for load in [*electrons, *fields[:1], *tables, *fields[1:]]:
        load.start()

    for t in range(slices):
        s = (y + t) % slices
        if t == 0:
            for load in electrons:
                load.wait()
        fields[t].wait()
        driven = push(
            s, me * rows, field_ref, phase_ref, energy_ref, row_ref, col_ref, phase_out, energy_out
        )
        if t == 0:
            for table in tables:
                table.wait()
        real, imag = turn_columns(driven, high_ref, low_ref)
        turned[s, 0] = real
        turned[s, 1] = imag
        if t == 0:
            peers = jnp.where(cut < n_cuts - 1, n_strip - 1 + n_strip // slices, n_strip - 1)
            pl.semaphore_wait(barrier, peers)

        for da in range(groups):
            for db in range(2):
                a = (y // slices + da) % groups
                e = (b + db) % 2
                target = (a * slices + s) * 2 + e
                lanes = pl.ds(pl.multiple_of((a * 2 + e) * quarter, quarter), quarter)
                source = turned.at[s, :, :, lanes]
                place = received.at[:, pl.ds(pl.multiple_of(me * rows, rows), rows), :]
                def send(to_cut):
                    pltpu.make_async_remote_copy(
                        src_ref=source,
                        dst_ref=place,
                        send_sem=go_send.at[t, da * 2 + db],
                        recv_sem=go_recv.at[me],
                        device_id={"cuts": to_cut, "strip": target},
                        device_id_type=MESH,
                    ).start()

                @pl.when((s == slices - 1) & (cut < n_cuts - 1))
                def _():
                    send(cut + 1)

                @pl.when(s < slices - 1)
                def _():
                    if t == 0 and da == 0 and db == 0:
                        pltpu.make_async_copy(source, place, go_recv.at[me]).start()
                    else:
                        send(cut)

    has_slice = jnp.logical_not(last) | (cut > 0)

    @pl.when(has_slice)
    def _():
        near = [0]
        for d in range(1, half // 2):
            near += [d, half - d]
        for d in near + [half // 2]:
            for db in range(2):
                i = (y + d) % half * 2 + (b + db) % 2
                block = pl.ds(pl.multiple_of(i * rows, rows), rows)
                place = received.at[:, block, :]
                pltpu.make_async_copy(place, place, go_recv.at[i]).wait()
                for part in range(2):
                    lanes = pl.ds(part * quarter, quarter)
                    upper, lower = split(received[part, block, :])
                    upper_half[block, lanes] = upper
                    lower_half[block, lanes] = lower

    @pl.when(jnp.logical_not(has_slice))
    def _():
        upper_half[...] = jnp.zeros(upper_half.shape, BF16)
        lower_half[...] = jnp.zeros(lower_half.shape, BF16)

    high = upper_half[...]
    low = lower_half[...]
    here = pl.ds(pl.multiple_of(my_quarter * quarter, quarter), quarter)
    steps = [half // 2]
    for d in range(half // 2 - 1, 0, -1):
        steps += [d, half - d]
    steps += [0]
    span = 2 * rows
    total_rows = high_ref.shape[0]
    for d in steps:
        to_y = (y + d) % half
        chunk = pl.ds(pl.multiple_of(to_y * span, span), span)
        factors = jnp.concatenate(
            [
                high_ref[chunk, :total_rows],
                high_ref[chunk, total_rows:],
                low_ref[chunk, :total_rows],
                low_ref[chunk, total_rows:],
            ],
            axis=0,
        )
        upper = dot(factors, high)
        total = upper[: 2 * span] + upper[2 * span :] + dot(factors[: 2 * span], low)
        mixed[0, chunk, :] = total[:span, :quarter] - total[span:, quarter:]
        mixed[1, chunk, :] = total[:span, quarter:] + total[span:, :quarter]
        for db in range(2):
            e = (b + db) % 2
            target = to_y * 2 + e
            source = mixed.at[:, pl.ds(pl.multiple_of(target * rows, rows), rows), :]

            place = out_ref.at[(my_slice + 1) % slices, :, :, here]
            if d == 0 and db == 0:
                pltpu.make_async_copy(source, place, back_recv.at[me]).start()
            else:
                pltpu.make_async_remote_copy(
                    src_ref=source,
                    dst_ref=place,
                    send_sem=back_send.at[d * 2 + db],
                    recv_sem=back_recv.at[me],
                    device_id={"cuts": cut, "strip": target},
                    device_id_type=MESH,
                ).start()

    block = received.at[:, pl.ds(0, rows), :]
    for t in range(slices):
        s = (y + t) % slices
        for k in range(n_strip // slices):
            goes = (s == slices - 1) & (cut < n_cuts - 1)
            if t > 0 or k > 0:
                goes = goes | (s < slices - 1)

            @pl.when(goes)
            def _():
                pltpu.make_async_copy(block, block, go_send.at[t, k]).wait()

    for i in range(n_strip):
        lanes = pl.ds(((i // 2) // slices * 2 + i % 2) * quarter, quarter)
        block = out_ref.at[((i // 2) % slices + 1) % slices, :, :, lanes]
        pltpu.make_async_copy(block, block, back_recv.at[i]).wait()
    block = mixed.at[:, pl.ds(0, rows), :]
    for k in range(1, n_strip):
        pltpu.make_async_copy(block, block, back_send.at[k]).wait()


def hand_out(field, phase, energy, field_out, phase_out, energy_out, sem):
    copies = [
        pltpu.make_async_copy(a, b, sem.at[i])
        for i, (a, b) in enumerate(
            ((field, field_out), (phase, phase_out), (energy, energy_out))
        )
    ]
    for copy in copies:
        copy.start()
    for copy in copies:
        copy.wait()


def shards(n_cuts, n_strip, field, phase, energy, row_bin, col_bin):
    slices, _, rows, cols = field.shape
    high, low = axis_matrix(cols)
    quarter = cols * slices // n_strip
    vmem = pl.BlockSpec(memory_space=pltpu.VMEM)
    dma = pltpu.SemaphoreType.DMA
    moved = pl.pallas_call(
        functools.partial(kernel, n_cuts, n_strip),
        out_shape=(
            pltpu.VMEM(field.shape, F32),
            pltpu.VMEM(phase.shape, F32),
            pltpu.VMEM(energy.shape, F32),
        ),
        in_specs=[pl.BlockSpec(memory_space=pl.ANY)] * 7,
        out_specs=(vmem,) * 3,
        scratch_shapes=[
            *(pltpu.VMEM(x.shape, x.dtype) for x in (field, phase, energy, row_bin, col_bin)),
            pltpu.VMEM(high.shape, BF16),
            pltpu.VMEM(low.shape, BF16),
            pltpu.VMEM(field.shape, F32),
            pltpu.VMEM((2, rows * n_strip, quarter), F32),
            pltpu.VMEM((rows * n_strip, 2 * quarter), BF16),
            pltpu.VMEM((rows * n_strip, 2 * quarter), BF16),
            pltpu.VMEM((2, rows * n_strip, quarter), F32),
            dma((6,)),
            dma((slices,)),
            dma((slices, n_strip // slices)),
            dma((n_strip,)),
            dma((n_strip,)),
            dma((n_strip,)),
        ],
        compiler_params=pltpu.CompilerParams(collective_id=0, has_side_effects=True),
    )(field, phase, energy, row_bin, col_bin, jnp.asarray(high), jnp.asarray(low))
    return pl.pallas_call(
        hand_out,
        out_shape=tuple(jax.ShapeDtypeStruct(x.shape, x.dtype) for x in moved),
        in_specs=[pl.BlockSpec(memory_space=pltpu.VMEM)] * 3,
        out_specs=(pl.BlockSpec(memory_space=pl.ANY),) * 3,
        scratch_shapes=[dma((3,))],
    )(*(pltpu.with_memory_space_constraint(x, pltpu.VMEM) for x in moved))


def solution(mesh):
    return jax.shard_map(
        functools.partial(shards, mesh.shape["cuts"], mesh.shape["strip"]),
        mesh=mesh,
        in_specs=(
            P("cuts", None, "strip", None),
            P("cuts", "strip"),
            P("cuts", "strip"),
            P("cuts", "strip"),
            P("cuts", "strip"),
        ),
        out_specs=(P("cuts", None, "strip", None), P("cuts", "strip"), P("cuts", "strip")),
        check_vma=False,
    )
```

```python
import functools
import math

import jax
import jax.numpy as jnp
import ml_dtypes
import numpy as np
from jax import lax
from jax.experimental import pallas as pl
from jax.experimental.pallas import tpu as pltpu
from jax.sharding import PartitionSpec as P

COUPLING = 0.5
DETUNING = 1.0
SOURCE_GAIN = 0.5
CHIRP_TOP = 60.0
MESH = pl.DeviceIdType.MESH
F32 = jnp.float32
BF16 = jnp.bfloat16


def axis_matrix(length):
    k = np.arange(length)
    q = np.where(k < length // 2, k, k - length) / (length // 2)
    response = np.fft.ifft(np.exp(-1j * CHIRP_TOP * q * q))
    matrix = response[(k[:, None] - k[None, :]) % length]
    both = np.concatenate([matrix.real, matrix.imag], axis=1).astype(np.float32)
    high = both.astype(ml_dtypes.bfloat16)
    low = (both - high.astype(np.float32)).astype(ml_dtypes.bfloat16)
    return high, low


def cos_sin(x):
    n = jnp.floor(x * (2.0 / math.pi) + 0.5)
    r = ((x - n * 1.5703125) - n * 4.837512969970703125e-4) - n * 7.549789948768648e-8
    z = r * r
    s = r + r * z * (-1.6666654611e-1 + z * (8.3321608736e-3 + z * -1.9515295891e-4))
    c = 1.0 - 0.5 * z + z * z * (
        4.166664568298827e-2 + z * (-1.388731625493765e-3 + z * 2.443315711809948e-5)
    )
    turn = n.astype(jnp.int32) & 3
    odd = (turn & 1) == 1
    cosine = jnp.where(odd, s, c)
    sine = jnp.where(odd, c, s)
    cosine = jnp.where((turn == 1) | (turn == 2), -cosine, cosine)
    sine = jnp.where(turn >= 2, -sine, sine)
    return cosine, sine


def split(x):
    high = x.astype(BF16)
    return high, (x - high.astype(F32)).astype(BF16)


def dot(a, b):
    return jnp.dot(a, b, preferred_element_type=F32)


def push(s, first_row, field_ref, phase_ref, energy_ref, row_ref, col_ref, phase_out, energy_out):
    rows = field_ref.shape[2]
    cols = field_ref.shape[3]
    count = phase_ref.shape[1]
    one = pl.ds(s, 1)
    field = field_ref[s].reshape(2 * rows, cols)
    phase = phase_ref[one, :]
    col_hot = jnp.where(
        lax.broadcasted_iota(jnp.int32, (cols, count), 0) == col_ref[one, :], 1.0, 0.0
    ).astype(BF16)
    row_hot = lax.broadcasted_iota(jnp.int32, (rows, count), 0) == row_ref[one, :] - first_row
    picked = dot(field.astype(BF16), col_hot)
    at_real = jnp.sum(jnp.where(row_hot, picked[:rows], 0.0), axis=0, keepdims=True)
    at_imag = jnp.sum(jnp.where(row_hot, picked[rows:], 0.0), axis=0, keepdims=True)
    cosine, sine = cos_sin(phase)
    energy_next = energy_ref[one, :] - COUPLING * (at_real * cosine - at_imag * sine)
    phase_next = phase + DETUNING * energy_next
    energy_out[one, :] = energy_next
    phase_out[one, :] = phase_next
    cosine, sine = cos_sin(phase_next)
    spread = jnp.concatenate(
        [jnp.where(row_hot, cosine, 0.0), jnp.where(row_hot, -sine, 0.0)], axis=0
    ).astype(BF16)
    deposit = lax.dot_general(spread, col_hot, (((1,), (1,)), ((), ())), preferred_element_type=F32)
    return field + SOURCE_GAIN * deposit


def turn_columns(driven, high_ref, low_ref):
    rows = driven.shape[0] // 2
    cols = driven.shape[1]
    high, low = split(driven)
    upper = dot(jnp.concatenate([high, low], axis=0), high_ref[...])
    total = upper[: 2 * rows] + upper[2 * rows :] + dot(high, low_ref[...])
    real = total[:rows, :cols] - total[rows:, cols:]
    imag = total[:rows, cols:] + total[rows:, :cols]
    return real, imag


def kernel(
    n_cuts,
    n_strip,
    field_in,
    phase_in,
    energy_in,
    row_in,
    col_in,
    high_in,
    low_in,
    out_ref,
    phase_out,
    energy_out,
    field_ref,
    phase_ref,
    energy_ref,
    row_ref,
    col_ref,
    high_ref,
    low_ref,
    turned,
    received,
    mixed,
    landed,
    load_sem,
    field_sem,
    go_send,
    go_recv,
    back_send,
    back_recv,
):
    slices, _, rows, cols = field_in.shape
    quarter = cols * slices // n_strip
    half = n_strip // 2
    groups = half // slices
    cut = lax.axis_index("cuts")
    me = lax.axis_index("strip")
    y, b = me // 2, me % 2
    my_slice = y % slices
    my_quarter = (y // slices) * 2 + b
    last = my_slice == slices - 1

    barrier = pltpu.get_barrier_semaphore()
    for d in range(1, n_strip):
        pl.semaphore_signal(
            barrier, inc=1, device_id={"cuts": cut, "strip": (me + d) % n_strip}, device_id_type=MESH
        )

    @pl.when(last & (cut > 0))
    def _():
        for i in range(n_strip):
            pl.semaphore_signal(
                barrier, inc=1, device_id={"cuts": cut - 1, "strip": i}, device_id_type=MESH
            )

    electrons = [
        pltpu.make_async_copy(a, b, load_sem.at[i])
        for i, (a, b) in enumerate(
            (
                (phase_in, phase_ref),
                (energy_in, energy_ref),
                (row_in, row_ref),
                (col_in, col_ref),
            )
        )
    ]
    fields = [
        pltpu.make_async_copy(
            field_in.at[(y + t) % slices], field_ref.at[(y + t) % slices], field_sem.at[t]
        )
        for t in range(slices)
    ]
    tables = [
        pltpu.make_async_copy(high_in, high_ref, load_sem.at[4]),
        pltpu.make_async_copy(low_in, low_ref, load_sem.at[5]),
    ]
    for load in [*electrons, *fields[:1], *tables, *fields[1:]]:
        load.start()

    def send_slice(t, h):
        s = (y + t) % slices
        for da in range(groups):
            for db in range(2):
                a = (y // slices + da) % groups
                e = (b + db) % 2
                target = (a * slices + s) * 2 + e
                lanes = pl.ds(pl.multiple_of((a * 2 + e) * quarter, quarter), quarter)
                source = turned.at[s, h, :, lanes]
                place = received.at[h, pl.ds(pl.multiple_of(me * rows, rows), rows), :]

                def send(to_cut):
                    pltpu.make_async_remote_copy(
                        src_ref=source,
                        dst_ref=place,
                        send_sem=go_send.at[h, t, da * 2 + db],
                        recv_sem=go_recv.at[h, me],
                        device_id={"cuts": to_cut, "strip": target},
                        device_id_type=MESH,
                    ).start()

                @pl.when((s == slices - 1) & (cut < n_cuts - 1))
                def _():
                    send(cut + 1)

                @pl.when(s < slices - 1)
                def _():
                    if t == 0 and da == 0 and db == 0:
                        pltpu.make_async_copy(source, place, go_recv.at[h, me]).start()
                    else:
                        send(cut)

    left = lax.broadcasted_iota(jnp.int32, (rows, quarter), 1) < quarter // 2

    def pick(x, z):
        return jnp.where(left, x, z)

    def turn(x):
        return pltpu.roll(x, quarter // 2, 1)

    for t in range(slices):
        s = (y + t) % slices
        if t == 0:
            for load in electrons:
                load.wait()
        fields[t].wait()
        driven = push(
            s, me * rows, field_ref, phase_ref, energy_ref, row_ref, col_ref, phase_out, energy_out
        )
        if t == 0:
            for table in tables:
                table.wait()
        real, imag = turn_columns(driven, high_ref, low_ref)
        for q in range(cols // quarter):
            lanes = pl.ds(q * quarter, quarter)
            re = real[:, q * quarter : (q + 1) * quarter]
            im = imag[:, q * quarter : (q + 1) * quarter]
            turned[s, 0, :, lanes] = pick(re, turn(im))
            turned[s, 1, :, lanes] = pick(turn(re), im)
        if t == 0:
            peers = jnp.where(cut < n_cuts - 1, n_strip - 1 + n_strip // slices, n_strip - 1)
            pl.semaphore_wait(barrier, peers)

        send_slice(t, 0)
    for t in range(slices):
        send_slice(t, 1)

    has_slice = jnp.logical_not(last) | (cut > 0)

    steps = [half // 2]
    for d in range(half // 2 - 1, 0, -1):
        steps += [d, half - d]
    steps += [0]
    span = 2 * rows
    total_rows = high_ref.shape[0]
    first_half = lax.broadcasted_iota(jnp.int32, (span, quarter), 1) < quarter // 2

    for h in range(2):

        @pl.when(has_slice)
        def _():
            for i in range(n_strip):
                block = received.at[h, pl.ds(i * rows, rows), :]
                pltpu.make_async_copy(block, block, go_recv.at[h, i]).wait()

        @pl.when(jnp.logical_not(has_slice))
        def _():
            received[h] = jnp.zeros((total_rows, quarter), F32)

        both = jnp.concatenate(split(received[h]), axis=1)
        for d in steps:
            to_y = (y + d) % half
            chunk = pl.ds(pl.multiple_of(to_y * span, span), span)
            factors = jnp.concatenate(
                [
                    high_ref[chunk, :total_rows],
                    high_ref[chunk, total_rows:],
                    low_ref[chunk, :total_rows],
                    low_ref[chunk, total_rows:],
                ],
                axis=0,
            )
            upper = dot(factors, both)
            total = (
                upper[: 2 * span, :quarter]
                + upper[2 * span :, :quarter]
                + upper[: 2 * span, quarter:]
            )
            cross = turn(total[span:])
            mixed[h, chunk, :] = total[:span] + jnp.where(first_half, -cross, cross)
            for db in range(2):
                target = to_y * 2 + (b + db) % 2
                source = mixed.at[h, pl.ds(pl.multiple_of(target * rows, rows), rows), :]
                place = landed.at[(my_slice + 1) % slices, my_quarter, h]
                if d == 0 and db == 0:
                    pltpu.make_async_copy(source, place, back_recv.at[h, me]).start()
                else:
                    pltpu.make_async_remote_copy(
                        src_ref=source,
                        dst_ref=place,
                        send_sem=back_send.at[h, d * 2 + db],
                        recv_sem=back_recv.at[h, me],
                        device_id={"cuts": cut, "strip": target},
                        device_id_type=MESH,
                    ).start()

    block = received.at[0, pl.ds(0, rows), :]
    for t in range(slices):
        s = (y + t) % slices
        for k in range(n_strip // slices):
            goes = (s == slices - 1) & (cut < n_cuts - 1)
            if t > 0 or k > 0:
                goes = goes | (s < slices - 1)

            @pl.when(goes)
            def _():
                for h in range(2):
                    pltpu.make_async_copy(block, block, go_send.at[h, t, k]).wait()

    for i in range(n_strip):
        slot, q = ((i // 2) % slices + 1) % slices, (i // 2) // slices * 2 + i % 2
        lanes = pl.ds(q * quarter, quarter)
        for h in range(2):
            place = landed.at[slot, q, h]
            pltpu.make_async_copy(place, place, back_recv.at[h, i]).wait()
        one, two = landed[slot, q, 0], landed[slot, q, 1]
        out_ref[slot, 0, :, lanes] = pick(one, turn(two))
        out_ref[slot, 1, :, lanes] = pick(turn(one), two)
    for k in range(1, n_strip):
        for h in range(2):
            pltpu.make_async_copy(block, block, back_send.at[h, k]).wait()


def hand_out(field, phase, energy, field_out, phase_out, energy_out, sem):
    copies = [
        pltpu.make_async_copy(a, b, sem.at[i])
        for i, (a, b) in enumerate(
            ((field, field_out), (phase, phase_out), (energy, energy_out))
        )
    ]
    for copy in copies:
        copy.start()
    for copy in copies:
        copy.wait()


def shards(n_cuts, n_strip, field, phase, energy, row_bin, col_bin):
    slices, _, rows, cols = field.shape
    high, low = axis_matrix(cols)
    quarter = cols * slices // n_strip
    vmem = pl.BlockSpec(memory_space=pltpu.VMEM)
    dma = pltpu.SemaphoreType.DMA
    moved = pl.pallas_call(
        functools.partial(kernel, n_cuts, n_strip),
        out_shape=(
            pltpu.VMEM(field.shape, F32),
            pltpu.VMEM(phase.shape, F32),
            pltpu.VMEM(energy.shape, F32),
        ),
        in_specs=[pl.BlockSpec(memory_space=pl.ANY)] * 7,
        out_specs=(vmem,) * 3,
        scratch_shapes=[
            *(pltpu.VMEM(x.shape, x.dtype) for x in (field, phase, energy, row_bin, col_bin)),
            pltpu.VMEM(high.shape, BF16),
            pltpu.VMEM(low.shape, BF16),
            pltpu.VMEM(field.shape, F32),
            pltpu.VMEM((2, rows * n_strip, quarter), F32),
            pltpu.VMEM((2, rows * n_strip, quarter), F32),
            pltpu.VMEM((slices, cols // quarter, 2, rows, quarter), F32),
            dma((6,)),
            dma((slices,)),
            dma((2, slices, n_strip // slices)),
            dma((2, n_strip)),
            dma((2, n_strip)),
            dma((2, n_strip)),
        ],
        compiler_params=pltpu.CompilerParams(collective_id=0, has_side_effects=True),
    )(field, phase, energy, row_bin, col_bin, jnp.asarray(high), jnp.asarray(low))
    return pl.pallas_call(
        hand_out,
        out_shape=tuple(jax.ShapeDtypeStruct(x.shape, x.dtype) for x in moved),
        in_specs=[pl.BlockSpec(memory_space=pltpu.VMEM)] * 3,
        out_specs=(pl.BlockSpec(memory_space=pl.ANY),) * 3,
        scratch_shapes=[dma((3,))],
    )(*(pltpu.with_memory_space_constraint(x, pltpu.VMEM) for x in moved))


def solution(mesh):
    return jax.shard_map(
        functools.partial(shards, mesh.shape["cuts"], mesh.shape["strip"]),
        mesh=mesh,
        in_specs=(
            P("cuts", None, "strip", None),
            P("cuts", "strip"),
            P("cuts", "strip"),
            P("cuts", "strip"),
            P("cuts", "strip"),
        ),
        out_specs=(P("cuts", None, "strip", None), P("cuts", "strip"), P("cuts", "strip")),
        check_vma=False,
    )
```

```python
import functools
import math

import jax
import jax.numpy as jnp
import ml_dtypes
import numpy as np
from jax import lax
from jax.experimental import pallas as pl
from jax.experimental.pallas import tpu as pltpu
from jax.sharding import PartitionSpec as P

COUPLING = 0.5
DETUNING = 1.0
SOURCE_GAIN = 0.5
CHIRP_TOP = 60.0
MESH = pl.DeviceIdType.MESH
F32 = jnp.float32
BF16 = jnp.bfloat16


def axis_matrix(length):
    k = np.arange(length)
    q = np.where(k < length // 2, k, k - length) / (length // 2)
    response = np.fft.ifft(np.exp(-1j * CHIRP_TOP * q * q))
    matrix = response[(k[:, None] - k[None, :]) % length]
    both = np.concatenate([matrix.real, matrix.imag], axis=1).astype(np.float32)
    high = both.astype(ml_dtypes.bfloat16)
    low = (both - high.astype(np.float32)).astype(ml_dtypes.bfloat16)
    return high, low


def cos_sin(x):
    n = jnp.floor(x * (2.0 / math.pi) + 0.5)
    r = ((x - n * 1.5703125) - n * 4.837512969970703125e-4) - n * 7.549789948768648e-8
    z = r * r
    s = r + r * z * (-1.6666654611e-1 + z * (8.3321608736e-3 + z * -1.9515295891e-4))
    c = 1.0 - 0.5 * z + z * z * (
        4.166664568298827e-2 + z * (-1.388731625493765e-3 + z * 2.443315711809948e-5)
    )
    turn = n.astype(jnp.int32) & 3
    odd = (turn & 1) == 1
    cosine = jnp.where(odd, s, c)
    sine = jnp.where(odd, c, s)
    cosine = jnp.where((turn == 1) | (turn == 2), -cosine, cosine)
    sine = jnp.where(turn >= 2, -sine, sine)
    return cosine, sine


def split(x):
    high = x.astype(BF16)
    return high, (x - high.astype(F32)).astype(BF16)


def dot(a, b):
    return jnp.dot(a, b, preferred_element_type=F32)


def push(s, first_row, field_ref, phase_ref, energy_ref, row_ref, col_ref, phase_out, energy_out):
    rows = field_ref.shape[2]
    cols = field_ref.shape[3]
    count = phase_ref.shape[1]
    one = pl.ds(s, 1)
    field = field_ref[s].reshape(2 * rows, cols)
    phase = phase_ref[one, :]
    col_hot = jnp.where(
        lax.broadcasted_iota(jnp.int32, (cols, count), 0) == col_ref[one, :], 1.0, 0.0
    ).astype(BF16)
    row_hot = lax.broadcasted_iota(jnp.int32, (rows, count), 0) == row_ref[one, :] - first_row
    picked = dot(field.astype(BF16), col_hot)
    at_real = jnp.sum(jnp.where(row_hot, picked[:rows], 0.0), axis=0, keepdims=True)
    at_imag = jnp.sum(jnp.where(row_hot, picked[rows:], 0.0), axis=0, keepdims=True)
    cosine, sine = cos_sin(phase)
    energy_next = energy_ref[one, :] - COUPLING * (at_real * cosine - at_imag * sine)
    phase_next = phase + DETUNING * energy_next
    energy_out[one, :] = energy_next
    phase_out[one, :] = phase_next
    cosine, sine = cos_sin(phase_next)
    spread = jnp.concatenate(
        [jnp.where(row_hot, cosine, 0.0), jnp.where(row_hot, -sine, 0.0)], axis=0
    ).astype(BF16)
    deposit = lax.dot_general(spread, col_hot, (((1,), (1,)), ((), ())), preferred_element_type=F32)
    return field + SOURCE_GAIN * deposit


def turn_columns(driven, high_ref, low_ref):
    rows = driven.shape[0] // 2
    cols = driven.shape[1]
    high, low = split(driven)
    upper = dot(jnp.concatenate([high, low], axis=0), high_ref[...])
    total = upper[: 2 * rows] + upper[2 * rows :] + dot(high, low_ref[...])
    real = total[:rows, :cols] - total[rows:, cols:]
    imag = total[:rows, cols:] + total[rows:, :cols]
    return real, imag


def kernel(
    n_cuts,
    n_strip,
    field_in,
    phase_in,
    energy_in,
    row_in,
    col_in,
    high_in,
    low_in,
    out_ref,
    phase_out,
    energy_out,
    field_ref,
    phase_ref,
    energy_ref,
    row_ref,
    col_ref,
    high_ref,
    low_ref,
    turned,
    received,
    mixed,
    landed,
    load_sem,
    field_sem,
    go_send,
    go_recv,
    back_send,
    back_recv,
):
    slices, _, rows, cols = field_in.shape
    quarter = cols * slices // n_strip
    half = n_strip // 2
    groups = half // slices
    cut = lax.axis_index("cuts")
    me = lax.axis_index("strip")
    y, b = me // 2, me % 2
    my_slice = y % slices
    my_quarter = (y // slices) * 2 + b
    last = my_slice == slices - 1

    barrier = pltpu.get_barrier_semaphore()
    for d in range(1, n_strip):
        pl.semaphore_signal(
            barrier, inc=1, device_id={"cuts": cut, "strip": (me + d) % n_strip}, device_id_type=MESH
        )

    @pl.when(last & (cut > 0))
    def _():
        for i in range(n_strip):
            pl.semaphore_signal(
                barrier, inc=1, device_id={"cuts": cut - 1, "strip": i}, device_id_type=MESH
            )

    electrons = [
        pltpu.make_async_copy(a, b, load_sem.at[i])
        for i, (a, b) in enumerate(
            (
                (phase_in, phase_ref),
                (energy_in, energy_ref),
                (row_in, row_ref),
                (col_in, col_ref),
            )
        )
    ]
    fields = [
        pltpu.make_async_copy(
            field_in.at[(y + t) % slices], field_ref.at[(y + t) % slices], field_sem.at[t]
        )
        for t in range(slices)
    ]
    tables = [
        pltpu.make_async_copy(high_in, high_ref, load_sem.at[4]),
        pltpu.make_async_copy(low_in, low_ref, load_sem.at[5]),
    ]
    for load in [*electrons, *fields[:1], *tables, *fields[1:]]:
        load.start()

    def send_slice(t, h):
        s = (y + t) % slices
        for da in range(groups):
            for db in range(2):
                a = (y // slices + da) % groups
                e = (b + db) % 2
                target = (a * slices + s) * 2 + e
                lanes = pl.ds(pl.multiple_of((a * 2 + e) * quarter, quarter), quarter)
                source = turned.at[s, h, :, lanes]
                place = received.at[h, pl.ds(pl.multiple_of(me * rows, rows), rows), :]

                def send(to_cut):
                    pltpu.make_async_remote_copy(
                        src_ref=source,
                        dst_ref=place,
                        send_sem=go_send.at[h, t, da * 2 + db],
                        recv_sem=go_recv.at[h, me],
                        device_id={"cuts": to_cut, "strip": target},
                        device_id_type=MESH,
                    ).start()

                @pl.when((s == slices - 1) & (cut < n_cuts - 1))
                def _():
                    send(cut + 1)

                @pl.when(s < slices - 1)
                def _():
                    if t == 0 and da == 0 and db == 0:
                        pltpu.make_async_copy(source, place, go_recv.at[h, me]).start()
                    else:
                        send(cut)

    left = lax.broadcasted_iota(jnp.int32, (rows, quarter), 1) < quarter // 2

    def pick(x, z):
        return jnp.where(left, x, z)

    def turn(x):
        return pltpu.roll(x, quarter // 2, 1)

    for t in range(slices):
        s = (y + t) % slices
        if t == 0:
            for load in electrons:
                load.wait()
        fields[t].wait()
        driven = push(
            s, me * rows, field_ref, phase_ref, energy_ref, row_ref, col_ref, phase_out, energy_out
        )
        if t == 0:
            for table in tables:
                table.wait()
        real, imag = turn_columns(driven, high_ref, low_ref)
        for q in range(cols // quarter):
            lanes = pl.ds(q * quarter, quarter)
            re = real[:, q * quarter : (q + 1) * quarter]
            im = imag[:, q * quarter : (q + 1) * quarter]
            turned[s, 0, :, lanes] = pick(re, turn(im))
            turned[s, 1, :, lanes] = pick(turn(re), im)
        if t == 0:
            peers = jnp.where(cut < n_cuts - 1, n_strip - 1 + n_strip // slices, n_strip - 1)
            pl.semaphore_wait(barrier, peers)

        send_slice(t, 0)
    for t in range(slices):
        send_slice(t, 1)

    has_slice = jnp.logical_not(last) | (cut > 0)

    steps = [half // 2]
    for d in range(half // 2 - 1, 0, -1):
        steps += [d, half - d]
    steps += [0]
    span = 2 * rows
    total_rows = high_ref.shape[0]
    first_half = lax.broadcasted_iota(jnp.int32, (span, quarter), 1) < quarter // 2

    for h in range(2):

        @pl.when(has_slice)
        def _():
            for i in range(n_strip):
                block = received.at[h, pl.ds(i * rows, rows), :]
                pltpu.make_async_copy(block, block, go_recv.at[h, i]).wait()

        @pl.when(jnp.logical_not(has_slice))
        def _():
            received[h] = jnp.zeros((total_rows, quarter), F32)

        both = jnp.concatenate(split(received[h]), axis=1)
        for d in steps:
            to_y = (y + d) % half
            chunk = pl.ds(pl.multiple_of(to_y * span, span), span)
            factors = jnp.concatenate(
                [
                    high_ref[chunk, :total_rows],
                    high_ref[chunk, total_rows:],
                    low_ref[chunk, :total_rows],
                    low_ref[chunk, total_rows:],
                ],
                axis=0,
            )
            upper = dot(factors, both)
            total = (
                upper[: 2 * span, :quarter]
                + upper[2 * span :, :quarter]
                + upper[: 2 * span, quarter:]
            )
            cross = turn(total[span:])
            mixed[h, chunk, :] = total[:span] + jnp.where(first_half, -cross, cross)
            for db in range(2):
                target = to_y * 2 + (b + db) % 2
                source = mixed.at[h, pl.ds(pl.multiple_of(target * rows, rows), rows), :]
                place = landed.at[(my_slice + 1) % slices, my_quarter, h]
                if d == 0 and db == 0:
                    pltpu.make_async_copy(source, place, back_recv.at[h, me]).start()
                else:
                    pltpu.make_async_remote_copy(
                        src_ref=source,
                        dst_ref=place,
                        send_sem=back_send.at[h, d * 2 + db],
                        recv_sem=back_recv.at[h, me],
                        device_id={"cuts": cut, "strip": target},
                        device_id_type=MESH,
                    ).start()

    block = received.at[0, pl.ds(0, rows), :]
    for t in range(slices):
        s = (y + t) % slices
        for k in range(n_strip // slices):
            goes = (s == slices - 1) & (cut < n_cuts - 1)
            if t > 0 or k > 0:
                goes = goes | (s < slices - 1)

            @pl.when(goes)
            def _():
                for h in range(2):
                    pltpu.make_async_copy(block, block, go_send.at[h, t, k]).wait()

    for d, db in [(d, db) for d in steps for db in range(2)]:
        from_y, e = (y - d + half) % half, (b + db) % 2
        i = from_y * 2 + e
        slot, q = (from_y % slices + 1) % slices, from_y // slices * 2 + e
        lanes = pl.ds(pl.multiple_of(q * quarter, quarter), quarter)
        for h in range(2):
            place = landed.at[slot, q, h]
            pltpu.make_async_copy(place, place, back_recv.at[h, i]).wait()
        one, two = landed[slot, q, 0], landed[slot, q, 1]
        out_ref[slot, 0, :, lanes] = pick(one, turn(two))
        out_ref[slot, 1, :, lanes] = pick(turn(one), two)
    for k in range(1, n_strip):
        for h in range(2):
            pltpu.make_async_copy(block, block, back_send.at[h, k]).wait()


def hand_out(field, phase, energy, field_out, phase_out, energy_out, sem):
    copies = [
        pltpu.make_async_copy(a, b, sem.at[i])
        for i, (a, b) in enumerate(
            (
                *((field.at[s], field_out.at[s]) for s in range(field.shape[0])),
                (phase, phase_out),
                (energy, energy_out),
            )
        )
    ]
    for copy in copies:
        copy.start()
    for copy in copies:
        copy.wait()


def shards(n_cuts, n_strip, field, phase, energy, row_bin, col_bin):
    slices, _, rows, cols = field.shape
    high, low = axis_matrix(cols)
    quarter = cols * slices // n_strip
    vmem = pl.BlockSpec(memory_space=pltpu.VMEM)
    dma = pltpu.SemaphoreType.DMA
    moved = pl.pallas_call(
        functools.partial(kernel, n_cuts, n_strip),
        out_shape=(
            pltpu.VMEM(field.shape, F32),
            pltpu.VMEM(phase.shape, F32),
            pltpu.VMEM(energy.shape, F32),
        ),
        in_specs=[pl.BlockSpec(memory_space=pl.ANY)] * 7,
        out_specs=(vmem,) * 3,
        scratch_shapes=[
            *(pltpu.VMEM(x.shape, x.dtype) for x in (field, phase, energy, row_bin, col_bin)),
            pltpu.VMEM(high.shape, BF16),
            pltpu.VMEM(low.shape, BF16),
            pltpu.VMEM(field.shape, F32),
            pltpu.VMEM((2, rows * n_strip, quarter), F32),
            pltpu.VMEM((2, rows * n_strip, quarter), F32),
            pltpu.VMEM((slices, cols // quarter, 2, rows, quarter), F32),
            dma((6,)),
            dma((slices,)),
            dma((2, slices, n_strip // slices)),
            dma((2, n_strip)),
            dma((2, n_strip)),
            dma((2, n_strip)),
        ],
        compiler_params=pltpu.CompilerParams(collective_id=0, has_side_effects=True),
    )(field, phase, energy, row_bin, col_bin, jnp.asarray(high), jnp.asarray(low))
    return pl.pallas_call(
        hand_out,
        out_shape=tuple(jax.ShapeDtypeStruct(x.shape, x.dtype) for x in moved),
        in_specs=[pl.BlockSpec(memory_space=pltpu.VMEM)] * 3,
        out_specs=(pl.BlockSpec(memory_space=pl.ANY),) * 3,
        scratch_shapes=[dma((slices + 2,))],
    )(*(pltpu.with_memory_space_constraint(x, pltpu.VMEM) for x in moved))


def solution(mesh):
    return jax.shard_map(
        functools.partial(shards, mesh.shape["cuts"], mesh.shape["strip"]),
        mesh=mesh,
        in_specs=(
            P("cuts", None, "strip", None),
            P("cuts", "strip"),
            P("cuts", "strip"),
            P("cuts", "strip"),
            P("cuts", "strip"),
        ),
        out_specs=(P("cuts", None, "strip", None), P("cuts", "strip"), P("cuts", "strip")),
        check_vma=False,
    )
```
